256 devices in a mesh: space: 32 (over y, z_hi, core), test: 2 (over z_lo), trial: 4 (over x).
Axes of the slice: x: 4, y: 4, z: 8 (z_hi: 4, z_lo: 2; z = z_hi * 2 + z_lo), core: 2. Of those that a mesh axis runs over, the one named last changes fastest.
Arguments:
- test_modes: bfloat16 [3, 128, 128, 8, 128], P(None, 'test', 'space'), may hold values from -6 to 6
- trial_modes: bfloat16 [3, 128, 128, 8, 128], P(None, 'trial', 'space'), may hold values from -6 to 6
- volumes: float32 [128, 8, 128], P('space'), may hold values from 0.25 to 4
Outputs:
- tensor: float32 [128, 128, 128], P('space', 'test', 'trial')
The draws below stay inside these ranges and needn't reach their ends.
All inputs are finite; a program needn't handle non-finite values.
Results may differ from the reference program's by a relative error of at most 0.0051.
Values may be sent and summed in bfloat16 or wider, within the bound.
No kernel may reach another device: no remote copies, remote signals or barrier semaphores. Data moves between devices by JAX's collectives and lax.ppermute only.
A program may use at most 64 MiB of HBM per device.

```python
import math
import jax
import jax.numpy as jnp
from jax import lax

R = 128
NY = 8
NZ = 128
NX = 128


def levels(rng, extent, shards, low, high):
    def one(dim, blocks):
        heights = jax.random.uniform(jax.random.fold_in(jax.random.fold_in(rng, 6), dim), (blocks,), jnp.float32, low / len(shards), high / len(shards))
        return jnp.repeat(jnp.exp(heights), extent[dim] // blocks).reshape((-1,) + (1,) * (len(extent) - dim - 1))

    factor_of = one(*shards[0])
    for cut in shards[1:]:
        factor_of = factor_of * one(*cut)
    return factor_of


def gaussian(stream_key, shape, width, most, cuts=(), dtype=jnp.bfloat16):
    values = width * jax.random.normal(stream_key, shape, jnp.float32)
    if cuts:
        values = values * levels(stream_key, shape, cuts, -0.22, 0.18)
    return jnp.clip(values, -most, most).astype(dtype)


def setup_inputs(seed: int = 0) -> dict:
    key_list = jax.random.split(jax.random.key(seed), 4)
    return {
        "test_modes": gaussian(key_list[0], (3, R, NX, NY, NZ), 1.0, 6.0, ((1, 2), (2, 32))),
        "trial_modes": gaussian(key_list[1], (3, R, NX, NY, NZ), 1.0, 6.0, ((1, 4), (2, 32))),
        "volumes": jnp.clip(jnp.exp(math.log(4.0) - 2.7725887 * jax.random.uniform(key_list[2], (NX, NY, NZ), jnp.float32) ** levels(key_list[2], (NX, NY, NZ), ((0, 32),), -0.2, 0.2)), 0.25, 4.0),
    }


def derivatives(padded):
    field = padded.astype(jnp.float32)
    along_x = (field[:, :, 2:] - field[:, :, :-2]) * 0.5
    center = field[:, :, 1:-1]
    wide_y = jnp.pad(center, ((0, 0), (0, 0), (0, 0), (1, 1), (0, 0)))
    along_y = (wide_y[:, :, :, 2:] - wide_y[:, :, :, :-2]) * 0.5
    wide_z = jnp.pad(center, ((0, 0), (0, 0), (0, 0), (0, 0), (1, 1)))
    along_z = (wide_z[:, :, :, :, 2:] - wide_z[:, :, :, :, :-2]) * 0.5
    return jnp.stack([along_x, along_y, along_z], axis=1).astype(jnp.bfloat16)

def reference(test_modes, trial_modes, volumes):
    cell_count = NX * NY * NZ
    padded = jnp.pad(trial_modes, ((0, 0), (0, 0), (1, 1), (0, 0), (0, 0)))
    gradients = derivatives(padded)
    weighted = (test_modes.astype(jnp.float32) * volumes).astype(jnp.bfloat16)

    def advance(position, running):
        plane = (position // NY).astype(jnp.int32)
        row = (position % NY).astype(jnp.int32)
        trial_block = lax.dynamic_index_in_dim(lax.dynamic_index_in_dim(trial_modes, plane, 2, False), row, 2, False).astype(jnp.float32)
        grad_block = lax.dynamic_index_in_dim(lax.dynamic_index_in_dim(gradients, plane, 3, False), row, 3, False).astype(jnp.float32)
        test_block = lax.dynamic_index_in_dim(lax.dynamic_index_in_dim(weighted, plane, 2, False), row, 2, False).astype(jnp.float32)
        convected = jnp.einsum('bjc,abkc->ajkc', trial_block, grad_block).astype(jnp.bfloat16)
        convected = lax.optimization_barrier(convected).astype(jnp.float32)
        return running + jnp.einsum('aic,ajkc->jik', test_block, convected)
    running = jnp.zeros((R, R, R), jnp.float32)
    running = lax.fori_loop(0, NX * NY, advance, running)
    return running * (1.0 / (4.0 * math.sqrt(cell_count)))
```

```python
import functools
import math

import jax
import jax.numpy as jnp
from jax import lax
from jax.experimental import pallas as pl
from jax.experimental.pallas import tpu as pltpu
from jax.sharding import PartitionSpec as P

F = jnp.float32
B = jnp.bfloat16
IB = 16


def kernel(w_ref, u0, u1, u2, u3, um, uc, up, out_ref, acc, gs, us, gb):
    step = pl.program_id(0)
    modes = u0.shape[3]
    tests = w_ref.shape[3]
    rows = uc.shape[1]
    lanes = uc.shape[4]
    y0 = 2 * (step % (rows // 2))
    lane = lax.broadcasted_iota(jnp.int32, (modes, lanes), 1)
    for yy in range(2):
        y = y0 + yy
        for a in range(3):
            c = uc[0, y, a].astype(F)
            gx = (up[0, y, a].astype(F) - um[0, y, a].astype(F)) * 0.5
            hi = jnp.where(y < rows - 1, uc[0, jnp.minimum(y + 1, rows - 1), a].astype(F), 0.0)
            lo = jnp.where(y > 0, uc[0, jnp.maximum(y - 1, 0), a].astype(F), 0.0)
            after = jnp.where(lane < lanes - 1, pltpu.roll(c, lanes - 1, 1), 0.0)
            before = jnp.where(lane > 0, pltpu.roll(c, 1, 1), 0.0)
            gs[yy, a, 0] = gx.astype(B)
            gs[yy, a, 1] = ((hi - lo) * 0.5).astype(B)
            gs[yy, a, 2] = ((after - before) * 0.5).astype(B)
    for q, u in enumerate((u0, u1, u2, u3)):
        for b in range(3):
            for yy in range(2):
                us[q * modes:(q + 1) * modes, (b * 2 + yy) * lanes:(b * 2 + yy + 1) * lanes] = u[0, yy, b]

    @pl.when(step == 0)
    def _():
        acc[...] = jnp.zeros_like(acc)

    def block(ib, carry):
        i0 = ib * IB
        for yy in range(2):
            g = [[[gs[yy, a, b, h:h + 16] for h in range(0, modes, 16)] for b in range(3)] for a in range(3)]
            for i in range(IB):
                wb = [jnp.broadcast_to(w_ref[0, yy, a, pl.ds(i0 + i, 1), :], (16, lanes)).astype(B) for a in range(3)]
                for b in range(3):
                    for h in range(modes // 16):
                        value = wb[0] * g[0][b][h] + wb[1] * g[1][b][h] + wb[2] * g[2][b][h]
                        row = i * modes + h * 16
                        gb[row:row + 16, (b * 2 + yy) * lanes:(b * 2 + yy + 1) * lanes] = value
        off = pl.multiple_of(i0 * modes, IB * modes)
        acc[pl.ds(off, IB * modes), :] += lax.dot_general(
            gb[...], us[...], (((1,), (1,)), ((), ())), preferred_element_type=F
        )
        return carry

    lax.fori_loop(0, tests // IB, block, 0)

    @pl.when(step == pl.num_programs(0) - 1)
    def _():
        out_ref[...] = acc[...].T


def compute(w, quarters, padded):
    planes, rows, _, tests, lanes = w.shape
    modes = padded.shape[3]
    pairs = rows // 2
    total = 4 * modes
    one = lambda s: (s // pairs, s % pairs, 0, 0, 0)
    quarter = pl.BlockSpec((1, 2, 3, modes, lanes), one)

    def plane(d):
        return pl.BlockSpec((1, rows, 3, modes, lanes), lambda s: (s // pairs + d, 0, 0, 0, 0))

    return pl.pallas_call(
        kernel,
        out_shape=jax.ShapeDtypeStruct((total, tests * modes), F),
        grid=(planes * pairs,),
        in_specs=[pl.BlockSpec((1, 2, 3, tests, lanes), one)] + [quarter] * 4 + [plane(0), plane(1), plane(2)],
        out_specs=pl.BlockSpec((total, tests * modes), lambda s: (0, 0)),
        scratch_shapes=[
            pltpu.VMEM((tests * modes, total), F),
            pltpu.VMEM((2, 3, 3, modes, lanes), B),
            pltpu.VMEM((total, 6 * lanes), B),
            pltpu.VMEM((IB * modes, 6 * lanes), B),
        ],
    )(w, *quarters, padded, padded, padded)


def exchange(parts, index, pairs, count):
    kept = lax.dynamic_index_in_dim(parts, index(0), 0, False)
    arrived = [
        lax.ppermute(lax.dynamic_index_in_dim(parts, index(d), 0, False).astype(B), "space", pairs(d))
        for d in range(1, count)
    ]
    for value in arrived:
        kept = kept + value.astype(F)
    return kept


def reduce_scatter(partial_value):
    total, width = partial_value.shape
    me = lax.axis_index("space")
    core, z, y = me % 2, (me // 2) % 4, me // 8
    x = lax.axis_index("trial")

    def where(y, z, core):
        return (y * 4 + z) * 2 + core

    every = [(y, z, c) for y in range(4) for z in range(4) for c in range(2)]
    along_core = lambda d: [(where(y, z, c), where(y, z, (c + d) % 2)) for y, z, c in every]
    along_y = lambda d: [(where(y, z, c), where((y + d) % 4, z, c)) for y, z, c in every]
    along_z = lambda d: [(where(y, z, c), where(y, (z + d) % 4, c)) for y, z, c in every]
    parts = partial_value.reshape(4, 4, 2, total // 32 * width // 128, 128).transpose(2, 0, 1, 3, 4)
    parts = exchange(parts, lambda d: (core + d) % 2, along_core, 2)
    parts = exchange(parts, lambda d: (y + d - x) % 4, along_y, 4)
    return exchange(parts, lambda d: (z + d) % 4, along_z, 4)


def shards(test_modes, trial_modes, volumes):
    planes = trial_modes.shape[2]
    modes = trial_modes.shape[1]
    tests = test_modes.shape[1]
    space = lax.axis_size("space")
    cell_count = planes * trial_modes.shape[3] * trial_modes.shape[4]
    factor = 1.0 / (4.0 * math.sqrt(cell_count * space))
    own = trial_modes.transpose(2, 3, 0, 1, 4)
    ring = lambda d: [(i, (i + d) % 4) for i in range(4)]
    left = lax.ppermute(own, "trial", ring(1))
    right = lax.ppermute(own, "trial", ring(-1))
    below = lax.ppermute(own[-1:], "space", [(i, i + 1) for i in range(space - 1)])
    above = lax.ppermute(own[:1], "space", [(i + 1, i) for i in range(space - 1)])
    padded = jnp.concatenate([below, own, above])
    weighted = (test_modes.astype(F) * volumes).transpose(2, 3, 0, 1, 4)
    half = planes // 2
    far = jnp.concatenate(
        [lax.ppermute(left[:half], "trial", ring(1)), lax.ppermute(right[half:], "trial", ring(-1))]
    )
    partial_value = compute(weighted, (own, right, far, left), padded)
    mine = reduce_scatter(partial_value)
    return mine.reshape(-1, tests, modes) * factor


def solution(mesh):
    return jax.shard_map(
        shards,
        mesh=mesh,
        in_specs=(
            P(None, "test", "space", None, None),
            P(None, "trial", "space", None, None),
            P("space", None, None),
        ),
        out_specs=P("space", "test", "trial"),
        check_vma=False,
    )
```

```python
import functools
import math

import jax
import jax.numpy as jnp
from jax import lax
from jax.experimental import pallas as pl
from jax.experimental.pallas import tpu as pltpu
from jax.sharding import PartitionSpec as P

F = jnp.float32
B = jnp.bfloat16
IB = 32
ANY = pl.BlockSpec(memory_space=pl.ANY)
HBM = pl.BlockSpec(memory_space=pltpu.HBM)
GROUPS = ((1, 2), (0,), (3,))


def kernel(plane, slot, first, last, *refs):
    test, volumes, own, right, left, far, below, here, above = refs[:9]
    refs = refs[9:]
    if not first:
        refs = refs[1:]
    if last:
        out, acc, wf, gs, near, us, gb, sems = refs
    else:
        acc, wf, gs, near, us, gb, sems = refs
    tests, rows, lanes = test.shape[1], test.shape[3], test.shape[4]
    modes = own.shape[3]
    lane = lax.broadcasted_iota(jnp.int32, (modes, lanes), 1)
    copies = [
        pltpu.make_async_copy(u.at[slot], us.at[:, :, pl.ds(q * modes, modes), :], sems.at[q])
        for q, u in enumerate((own, right, far, left))
    ]
    sides = [
        pltpu.make_async_copy(u.at[0], near.at[n], sems.at[4 + n]) for n, u in enumerate((below, above))
    ]
    for copy in sides + copies:
        copy.start()
    volume = volumes[plane]
    for a in range(3):
        wf[a] = test[a, :, plane].astype(F) * volume[None]
    if first:
        acc[...] = jnp.zeros_like(acc)

    def along_rows(y, carry):
        for a in range(3):
            hi = here[0, jnp.minimum(y + 1, rows - 1), a]
            lo = here[0, jnp.maximum(y - 1, 0), a]
            hi = jnp.where(y < rows - 1, hi, jnp.zeros_like(hi))
            lo = jnp.where(y > 0, lo, jnp.zeros_like(lo))
            gs[y, a, 1] = (hi - lo) * B(0.5)
            c = here[0, y, a].astype(F)
            after = jnp.where(lane < lanes - 1, pltpu.roll(c, lanes - 1, 1), 0.0)
            before = jnp.where(lane > 0, pltpu.roll(c, 1, 1), 0.0)
            gs[y, a, 2] = ((after - before) * 0.5).astype(B)
        return carry

    lax.fori_loop(0, rows, along_rows, 0)
    for copy in sides:
        copy.wait()

    def along_planes(y, carry):
        for a in range(3):
            gs[y, a, 0] = (near[1, y, a] - near[0, y, a]) * B(0.5)
        return carry

    lax.fori_loop(0, rows, along_planes, 0)
    for copy in copies:
        copy.wait()

    def pair(yp, carry):
        def block(ib, inner):
            i0 = ib * IB
            for yy in range(2):
                g = [[[gs[2 * yp + yy, a, b, h:h + 16] for h in range(0, modes, 16)] for b in range(3)] for a in range(3)]
                for i in range(IB):
                    wb = [
                        jnp.broadcast_to(wf[a, i0 + i, pl.ds(2 * yp + yy, 1), :], (16, lanes)).astype(B)
                        for a in range(3)
                    ]
                    for b in range(3):
                        for h in range(modes // 16):
                            value = wb[0] * g[0][b][h] + wb[1] * g[1][b][h] + wb[2] * g[2][b][h]
                            row = i * modes + h * 16
                            gb[b * 2 + yy, row:row + 16, :] = value
            off = pl.multiple_of(i0 * modes, IB * modes)
            acc[pl.ds(off, IB * modes), :] += lax.dot_general(
                jnp.concatenate([gb[t] for t in range(6)], axis=1),
                jnp.concatenate([us[2 * yp + yy, b] for b in range(3) for yy in range(2)], axis=1),
                (((1,), (1,)), ((), ())),
                preferred_element_type=F,
            )
            return inner

        return lax.fori_loop(0, tests // IB, block, carry)

    lax.fori_loop(0, rows // 2, pair, 0)
    if last:
        for m in range(out.shape[1]):
            turned = acc[m * lanes:(m + 1) * lanes, :].T
            for s in range(out.shape[0]):
                out[s, m] = turned[4 * s:4 * s + 4]


def compute(plane, slot, first, last, operands, running):
    test, own = operands[0], operands[2]
    tests, lanes = test.shape[1], test.shape[4]
    modes = own.shape[3]
    total = 4 * modes
    rows = tests * modes
    vmem = pl.BlockSpec(memory_space=pltpu.VMEM)
    acc = jax.ShapeDtypeStruct((rows, total), F)
    if last:
        out_shape = (jax.ShapeDtypeStruct((total // 4, rows // lanes, 4, lanes), F), acc)
        out_specs = (vmem, vmem)
    else:
        out_shape, out_specs = acc, vmem
    args = list(operands) + ([] if first else [running])
    work = 2 * tests * modes * total * 3 * test.shape[3] * lanes
    return pl.pallas_call(
        functools.partial(kernel, plane, slot, first, last),
        out_shape=out_shape,
        in_specs=[vmem] * 2 + [ANY] + [HBM] * 3 + [ANY, vmem, ANY] + [vmem] * (len(args) - 9),
        out_specs=out_specs,
        input_output_aliases={} if first else {len(args) - 1: 1 if last else 0},
        scratch_shapes=[
            pltpu.VMEM((3, tests, test.shape[3], lanes), F),
            pltpu.VMEM((test.shape[3], 3, 3, modes, lanes), B),
            pltpu.VMEM((2, test.shape[3], 3, modes, lanes), B),
            pltpu.VMEM((test.shape[3], 3, total, lanes), B),
            pltpu.VMEM((6, IB * modes, lanes), B),
            pltpu.SemaphoreType.DMA((6,)),
        ],
        compiler_params=pltpu.CompilerParams(vmem_limit_bytes=24 * 2**20),
        cost_estimate=pl.CostEstimate(flops=work, bytes_accessed=2**22, transcendentals=0),
        name=f"plane_{plane}",
    )(*args)


def exchange(parts, index, pairs, count):
    kept = lax.dynamic_index_in_dim(parts, index(0), 0, False)
    arrived = [
        lax.ppermute(lax.dynamic_index_in_dim(parts, index(d), 0, False).astype(B), "space", pairs(d))
        for d in range(1, count)
    ]
    for value in arrived:
        kept = kept + value.astype(F)
    return kept


def reduce_scatter(partial_value):
    me = lax.axis_index("space")
    core, z, y = me % 2, (me // 2) % 4, me // 8
    x = lax.axis_index("trial")

    def where(y, z, core):
        return (y * 4 + z) * 2 + core

    every = [(y, z, c) for y in range(4) for z in range(4) for c in range(2)]
    along_core = lambda d: [(where(y, z, c), where(y, z, (c + d) % 2)) for y, z, c in every]
    along_y = lambda d: [(where(y, z, c), where((y + d) % 4, z, c)) for y, z, c in every]
    along_z = lambda d: [(where(y, z, c), where(y, (z + d) % 4, c)) for y, z, c in every]
    parts = partial_value.reshape((4, 4, 2) + partial_value.shape[1:]).transpose(2, 0, 1, 3, 4, 5)
    parts = exchange(parts, lambda d: (core + d) % 2, along_core, 2)
    parts = exchange(parts, lambda d: (y + d - x) % 4, along_y, 4)
    return exchange(parts, lambda d: (z + d) % 4, along_z, 4)


def shards(test_modes, trial_modes, volumes):
    planes, rows = trial_modes.shape[2:4]
    modes = trial_modes.shape[1]
    tests = test_modes.shape[1]
    space = lax.axis_size("space")
    cell_count = planes * rows * trial_modes.shape[4]
    factor = 1.0 / (4.0 * math.sqrt(cell_count * space))
    own = trial_modes.transpose(2, 3, 0, 1, 4)
    up = [(i, (i + 1) % 4) for i in range(4)]
    down = [(i, (i - 1) % 4) for i in range(4)]
    across = [(i, (i + 2) % 4) for i in range(4)]
    gathered = []
    for group in GROUPS:
        block = own[group[0]:group[-1] + 1]
        gathered.append((block,) + tuple(lax.ppermute(block, "trial", pairs) for pairs in (down, across, up)))
    own = [own[p:p + 1] for p in range(planes)]
    below = lax.ppermute(own[-1], "space", [(i, i + 1) for i in range(space - 1)])
    above = lax.ppermute(own[0], "space", [(i + 1, i) for i in range(space - 1)])
    around = [below] + own + [above]
    running = None
    done = 0
    for group, (block, right, far, left) in zip(GROUPS, gathered):
        for slot, p in enumerate(group):
            operands = (test_modes, volumes, block, right, left, far) + tuple(around[p:p + 3])
            running = compute(p, slot, done == 0, done == planes - 1, operands, running)
            done += 1
    mine = reduce_scatter(running[0])
    return mine.transpose(1, 0, 2).reshape(-1, tests, modes) * factor


def solution(mesh):
    return jax.shard_map(
        shards,
        mesh=mesh,
        in_specs=(
            P(None, "test", "space", None, None),
            P(None, "trial", "space", None, None),
            P("space", None, None),
        ),
        out_specs=P("space", "test", "trial"),
        check_vma=False,
    )
```

```python
import functools
import math

import jax
import jax.numpy as jnp
from jax import lax
from jax.experimental import pallas as pl
from jax.experimental.pallas import tpu as pltpu
from jax.sharding import PartitionSpec as P

F = jnp.float32
B = jnp.bfloat16
IB = 64
ANY = pl.BlockSpec(memory_space=pl.ANY)
HBM = pl.BlockSpec(memory_space=pltpu.HBM)
GROUPS = ((1, 2), (0,), (3,))


def kernel(plane, slot, first, last, *refs):
    test, volumes, own, right, left, far, below, here, above = refs[:9]
    refs = refs[9:]
    if not first:
        refs = refs[1:]
    if last:
        out, acc, wf, gs, near, us, sems = refs
    else:
        acc, wf, gs, near, us, sems = refs
    tests, rows, lanes = test.shape[1], test.shape[3], test.shape[4]
    modes = own.shape[3]
    lane = lax.broadcasted_iota(jnp.int32, (modes, lanes), 1)
    copies = [
        pltpu.make_async_copy(u.at[slot], us.at[:, :, pl.ds(q * modes, modes), :], sems.at[q])
        for q, u in enumerate((own, right, far, left))
    ]
    sides = [
        pltpu.make_async_copy(u.at[0], near.at[n], sems.at[4 + n]) for n, u in enumerate((below, above))
    ]
    for copy in sides + copies:
        copy.start()
    volume = volumes[plane]
    for a in range(3):
        wf[a] = test[a, :, plane].astype(F) * volume[None]
    if first:
        acc[...] = jnp.zeros_like(acc)

    def along_rows(y, carry):
        for a in range(3):
            hi = here[0, jnp.minimum(y + 1, rows - 1), a]
            lo = here[0, jnp.maximum(y - 1, 0), a]
            hi = jnp.where(y < rows - 1, hi, jnp.zeros_like(hi))
            lo = jnp.where(y > 0, lo, jnp.zeros_like(lo))
            gs[y, a, 1] = (hi - lo) * B(0.5)
            c = here[0, y, a].astype(F)
            after = jnp.where(lane < lanes - 1, pltpu.roll(c, lanes - 1, 1), 0.0)
            before = jnp.where(lane > 0, pltpu.roll(c, 1, 1), 0.0)
            gs[y, a, 2] = ((after - before) * 0.5).astype(B)
        return carry

    lax.fori_loop(0, rows, along_rows, 0)
    for copy in sides:
        copy.wait()

    def along_planes(y, carry):
        for a in range(3):
            gs[y, a, 0] = (near[1, y, a] - near[0, y, a]) * B(0.5)
        return carry

    lax.fori_loop(0, rows, along_planes, 0)
    for copy in copies:
        copy.wait()

    def pair(yp, carry):
        def block(ib, inner):
            i0 = ib * IB
            columns = []
            for b in range(3):
                for yy in range(2):
                    y = 2 * yp + yy
                    g = [[gs[y, a, b, h:h + 16] for h in range(0, modes, 16)] for a in range(3)]
                    values = []
                    for i in range(IB):
                        wb = [
                            jnp.broadcast_to(wf[a, i0 + i, pl.ds(y, 1), :], (16, lanes)).astype(B)
                            for a in range(3)
                        ]
                        for h in range(modes // 16):
                            values.append(wb[0] * g[0][h] + wb[1] * g[1][h] + wb[2] * g[2][h])
                    columns.append(jnp.concatenate(values, axis=0))
            off = pl.multiple_of(i0 * modes, IB * modes)
            acc[pl.ds(off, IB * modes), :] += lax.dot_general(
                jnp.concatenate(columns, axis=1),
                jnp.concatenate([us[2 * yp + yy, b] for b in range(3) for yy in range(2)], axis=1),
                (((1,), (1,)), ((), ())),
                preferred_element_type=F,
            )
            return inner

        return lax.fori_loop(0, tests // IB, block, carry)

    lax.fori_loop(0, rows // 2, pair, 0)
    if last:
        for m in range(out.shape[1]):
            turned = acc[m * lanes:(m + 1) * lanes, :].T
            for s in range(out.shape[0]):
                out[s, m] = turned[4 * s:4 * s + 4]


def compute(plane, slot, first, last, operands, running):
    test, own = operands[0], operands[2]
    tests, lanes = test.shape[1], test.shape[4]
    modes = own.shape[3]
    total = 4 * modes
    rows = tests * modes
    vmem = pl.BlockSpec(memory_space=pltpu.VMEM)
    acc = jax.ShapeDtypeStruct((rows, total), F)
    if last:
        out_shape = (jax.ShapeDtypeStruct((total // 4, rows // lanes, 4, lanes), F), acc)
        out_specs = (vmem, vmem)
    else:
        out_shape, out_specs = acc, vmem
    args = list(operands) + ([] if first else [running])
    work = 2 * tests * modes * total * 3 * test.shape[3] * lanes
    return pl.pallas_call(
        functools.partial(kernel, plane, slot, first, last),
        out_shape=out_shape,
        in_specs=[vmem] * 2 + [ANY] + [HBM] * 3 + [ANY, vmem, ANY] + [vmem] * (len(args) - 9),
        out_specs=out_specs,
        input_output_aliases={} if first else {len(args) - 1: 1 if last else 0},
        scratch_shapes=[
            pltpu.VMEM((3, tests, test.shape[3], lanes), F),
            pltpu.VMEM((test.shape[3], 3, 3, modes, lanes), B),
            pltpu.VMEM((2, test.shape[3], 3, modes, lanes), B),
            pltpu.VMEM((test.shape[3], 3, total, lanes), B),
            pltpu.SemaphoreType.DMA((6,)),
        ],
        compiler_params=pltpu.CompilerParams(vmem_limit_bytes=24 * 2**20),
        cost_estimate=pl.CostEstimate(flops=work, bytes_accessed=2**22, transcendentals=0),
        name=f"plane_{plane}",
    )(*args)


def exchange(parts, index, pairs, count):
    kept = lax.dynamic_index_in_dim(parts, index(0), 0, False)
    arrived = [
        lax.ppermute(lax.dynamic_index_in_dim(parts, index(d), 0, False).astype(B), "space", pairs(d))
        for d in range(1, count)
    ]
    for value in arrived:
        kept = kept + value.astype(F)
    return kept


def reduce_scatter(partial_value):
    me = lax.axis_index("space")
    core, z, y = me % 2, (me // 2) % 4, me // 8
    x = lax.axis_index("trial")

    def where(y, z, core):
        return (y * 4 + z) * 2 + core

    every = [(y, z, c) for y in range(4) for z in range(4) for c in range(2)]
    along_core = lambda d: [(where(y, z, c), where(y, z, (c + d) % 2)) for y, z, c in every]
    along_y = lambda d: [(where(y, z, c), where((y + d) % 4, z, c)) for y, z, c in every]
    along_z = lambda d: [(where(y, z, c), where(y, (z + d) % 4, c)) for y, z, c in every]
    parts = partial_value.reshape((4, 4, 2) + partial_value.shape[1:]).transpose(2, 0, 1, 3, 4, 5)
    parts = exchange(parts, lambda d: (core + d) % 2, along_core, 2)
    parts = exchange(parts, lambda d: (y + d - x) % 4, along_y, 4)
    return exchange(parts, lambda d: (z + d) % 4, along_z, 4)


def shards(test_modes, trial_modes, volumes):
    planes, rows = trial_modes.shape[2:4]
    modes = trial_modes.shape[1]
    tests = test_modes.shape[1]
    space = lax.axis_size("space")
    cell_count = planes * rows * trial_modes.shape[4]
    factor = 1.0 / (4.0 * math.sqrt(cell_count * space))
    own = trial_modes.transpose(2, 3, 0, 1, 4)
    up = [(i, (i + 1) % 4) for i in range(4)]
    down = [(i, (i - 1) % 4) for i in range(4)]
    across = [(i, (i + 2) % 4) for i in range(4)]
    gathered = []
    for group in GROUPS:
        block = own[group[0]:group[-1] + 1]
        gathered.append((block,) + tuple(lax.ppermute(block, "trial", pairs) for pairs in (down, across, up)))
    own = [own[p:p + 1] for p in range(planes)]
    below = lax.ppermute(own[-1], "space", [(i, i + 1) for i in range(space - 1)])
    above = lax.ppermute(own[0], "space", [(i + 1, i) for i in range(space - 1)])
    around = [below] + own + [above]
    running = None
    done = 0
    for group, (block, right, far, left) in zip(GROUPS, gathered):
        for slot, p in enumerate(group):
            operands = (test_modes, volumes, block, right, left, far) + tuple(around[p:p + 3])
            running = compute(p, slot, done == 0, done == planes - 1, operands, running)
            done += 1
    mine = reduce_scatter(running[0])
    return mine.transpose(1, 0, 2).reshape(-1, tests, modes) * factor


def solution(mesh):
    return jax.shard_map(
        shards,
        mesh=mesh,
        in_specs=(
            P(None, "test", "space", None, None),
            P(None, "trial", "space", None, None),
            P("space", None, None),
        ),
        out_specs=P("space", "test", "trial"),
        check_vma=False,
    )
```

```python
import functools
import math

import jax
import jax.numpy as jnp
from jax import lax
from jax.experimental import pallas as pl
from jax.experimental.pallas import tpu as pltpu
from jax.sharding import PartitionSpec as P

F = jnp.float32
B = jnp.bfloat16
IB = 64
ANY = pl.BlockSpec(memory_space=pl.ANY)
HBM = pl.BlockSpec(memory_space=pltpu.HBM)
GROUPS = ((1, 2), (0,), (3,))


def kernel(plane, slot, first, last, *refs):
    test, volumes, own, right, left, far, below, here, above = refs[:9]
    refs = refs[9:]
    if not first:
        refs = refs[1:]
    if last:
        out, acc, wf, gs, near, us, sems = refs
    else:
        acc, wf, gs, near, us, sems = refs
    tests, rows, lanes = test.shape[1], test.shape[3], test.shape[4]
    modes = own.shape[3]
    lane = lax.broadcasted_iota(jnp.int32, (modes, lanes), 1)
    copies = [
        pltpu.make_async_copy(u.at[slot], us.at[:, :, pl.ds(q * modes, modes), :], sems.at[q])
        for q, u in enumerate((own, right, far, left))
    ]
    sides = [
        pltpu.make_async_copy(u.at[0], near.at[n], sems.at[4 + n]) for n, u in enumerate((below, above))
    ]
    for copy in sides + copies:
        copy.start()
    volume = volumes[plane]
    for a in range(3):
        wf[a] = test[a, :, plane].astype(F) * volume[None]
    if first:
        acc[...] = jnp.zeros_like(acc)

    def along_rows(y, carry):
        for a in range(3):
            hi = here[0, jnp.minimum(y + 1, rows - 1), a]
            lo = here[0, jnp.maximum(y - 1, 0), a]
            hi = jnp.where(y < rows - 1, hi, jnp.zeros_like(hi))
            lo = jnp.where(y > 0, lo, jnp.zeros_like(lo))
            gs[y, a, 1] = (hi - lo) * B(0.5)
            c = here[0, y, a].astype(F)
            after = jnp.where(lane < lanes - 1, pltpu.roll(c, lanes - 1, 1), 0.0)
            before = jnp.where(lane > 0, pltpu.roll(c, 1, 1), 0.0)
            gs[y, a, 2] = ((after - before) * 0.5).astype(B)
        return carry

    lax.fori_loop(0, rows, along_rows, 0)
    for copy in sides:
        copy.wait()

    def along_planes(y, carry):
        for a in range(3):
            gs[y, a, 0] = (near[1, y, a] - near[0, y, a]) * B(0.5)
        return carry

    lax.fori_loop(0, rows, along_planes, 0)
    for copy in copies:
        copy.wait()

    def pair(yp, carry):
        def block(ib, inner):
            i0 = ib * IB
            columns = []
            for b in range(3):
                for yy in range(2):
                    y = 2 * yp + yy
                    g = [[gs[y, a, b, h:h + 16] for h in range(0, modes, 16)] for a in range(3)]
                    values = []
                    for i in range(IB):
                        wb = [
                            jnp.broadcast_to(wf[a, i0 + i, pl.ds(y, 1), :], (16, lanes)).astype(B)
                            for a in range(3)
                        ]
                        for h in range(modes // 16):
                            values.append(wb[0] * g[0][h] + wb[1] * g[1][h] + wb[2] * g[2][h])
                    columns.append(jnp.concatenate(values, axis=0))
            off = pl.multiple_of(i0 * modes, IB * modes)
            acc[pl.ds(off, IB * modes), :] += lax.dot_general(
                jnp.concatenate(columns, axis=1),
                jnp.concatenate([us[2 * yp + yy, b] for b in range(3) for yy in range(2)], axis=1),
                (((1,), (1,)), ((), ())),
                preferred_element_type=F,
            )
            return inner

        return lax.fori_loop(0, tests // IB, block, carry)

    lax.fori_loop(0, rows // 2, pair, 0)
    if last:
        for m in range(out.shape[1]):
            turned = acc[m * lanes:(m + 1) * lanes, :].T
            for s in range(out.shape[0]):
                out[s, m] = turned[4 * s:4 * s + 4]


def compute(plane, slot, first, last, operands, running):
    test, own = operands[0], operands[2]
    tests, lanes = test.shape[1], test.shape[4]
    modes = own.shape[3]
    total = 4 * modes
    rows = tests * modes
    vmem = pl.BlockSpec(memory_space=pltpu.VMEM)
    acc = jax.ShapeDtypeStruct((rows, total), F)
    if last:
        out_shape = (jax.ShapeDtypeStruct((total // 4, rows // lanes, 4, lanes), F), acc)
        out_specs = (vmem, vmem)
    else:
        out_shape, out_specs = acc, vmem
    args = list(operands) + ([] if first else [running])
    work = 2 * tests * modes * total * 3 * test.shape[3] * lanes
    return pl.pallas_call(
        functools.partial(kernel, plane, slot, first, last),
        out_shape=out_shape,
        in_specs=[vmem] * 2 + [ANY] + [HBM] * 3 + [ANY, vmem, ANY] + [vmem] * (len(args) - 9),
        out_specs=out_specs,
        input_output_aliases={} if first else {len(args) - 1: 1 if last else 0},
        scratch_shapes=[
            pltpu.VMEM((3, tests, test.shape[3], lanes), F),
            pltpu.VMEM((test.shape[3], 3, 3, modes, lanes), B),
            pltpu.VMEM((2, test.shape[3], 3, modes, lanes), B),
            pltpu.VMEM((test.shape[3], 3, total, lanes), B),
            pltpu.SemaphoreType.DMA((6,)),
        ],
        compiler_params=pltpu.CompilerParams(vmem_limit_bytes=24 * 2**20),
        cost_estimate=pl.CostEstimate(flops=work, bytes_accessed=2**22, transcendentals=0),
        name=f"plane_{plane}",
    )(*args)


def exchange(parts, index, pairs, count):
    kept = lax.dynamic_index_in_dim(parts, index(0), 0, False)
    arrived = [
        lax.ppermute(lax.dynamic_index_in_dim(parts, index(d), 0, False).astype(B), "space", pairs(d))
        for d in range(1, count)
    ]
    for value in arrived:
        kept = kept + value.astype(F)
    return kept


def reduce_scatter(partial_value):
    me = lax.axis_index("space")
    core, z, y = me % 2, (me // 2) % 4, me // 8
    x = lax.axis_index("trial")

    def where(y, z, core):
        return (y * 4 + z) * 2 + core

    every = [(y, z, c) for y in range(4) for z in range(4) for c in range(2)]
    along_core = lambda d: [(where(y, z, c), where(y, z, (c + d) % 2)) for y, z, c in every]
    along_y = lambda d: [(where(y, z, c), where((y + d) % 4, z, c)) for y, z, c in every]
    along_z = lambda d: [(where(y, z, c), where(y, (z + d) % 4, c)) for y, z, c in every]
    parts = partial_value.reshape((4, 4, 2) + partial_value.shape[1:]).transpose(2, 0, 1, 3, 4, 5)
    parts = exchange(parts, lambda d: (core + d) % 2, along_core, 2)
    parts = exchange(parts, lambda d: (y + d - x) % 4, along_y, 4)
    return exchange(parts, lambda d: (z + d) % 4, along_z, 4)


def shards(test_modes, trial_modes, volumes):
    planes, rows = trial_modes.shape[2:4]
    modes = trial_modes.shape[1]
    tests = test_modes.shape[1]
    space = lax.axis_size("space")
    cell_count = planes * rows * trial_modes.shape[4]
    factor = 1.0 / (4.0 * math.sqrt(cell_count * space))
    own = trial_modes.transpose(2, 3, 0, 1, 4)
    up = [(i, (i + 1) % 4) for i in range(4)]
    down = [(i, (i - 1) % 4) for i in range(4)]
    across = [(i, (i + 2) % 4) for i in range(4)]
    gathered = []
    for group in GROUPS:
        block = own[group[0]:group[-1] + 1]
        gathered.append((block,) + tuple(lax.ppermute(block, "trial", pairs) for pairs in (down, across, up)))
    own = [own[p:p + 1] for p in range(planes)]
    below = lax.ppermute(own[-1], "space", [(i, i + 1) for i in range(space - 1)])
    above = lax.ppermute(own[0], "space", [(i + 1, i) for i in range(space - 1)])
    below, above = lax.optimization_barrier((below, above))
    around = [below] + own + [above]
    running = None
    done = 0
    for group, (block, right, far, left) in zip(GROUPS, gathered):
        for slot, p in enumerate(group):
            operands = (test_modes, volumes, block, right, left, far) + tuple(around[p:p + 3])
            running = compute(p, slot, done == 0, done == planes - 1, operands, running)
            done += 1
    mine = reduce_scatter(running[0])
    return mine.transpose(1, 0, 2).reshape(-1, tests, modes) * factor


def solution(mesh):
    return jax.shard_map(
        shards,
        mesh=mesh,
        in_specs=(
            P(None, "test", "space", None, None),
            P(None, "trial", "space", None, None),
            P("space", None, None),
        ),
        out_specs=P("space", "test", "trial"),
        check_vma=False,
    )
```
